32 devices in a mesh: dp: 16 (over z, y, core), fsdp: 2 (over x).
Axes of the slice: x: 2, y: 2, z: 4, core: 2. Of those that a mesh axis runs over, the one named last changes fastest.
Arguments:
- hidden_in: bfloat16 [16384, 1024], P(('dp', 'fsdp')), may hold values from -6 to 6
- cotangent: bfloat16 [16384, 1024], P(('dp', 'fsdp')), may hold values from -6 to 6
- seq_lens: int32 [16, 4], P('dp'), may hold values from 0 to 1024, as said below
- w_qkv: bfloat16 [1024, 3, 1024], P('dp', None, 'fsdp'), may hold values from -0.1875 to 0.1875
- qv_bias: bfloat16 [2048], P(('dp', 'fsdp')), may hold values from -3 to 3
- w_out: bfloat16 [1024, 1024], P('fsdp', 'dp'), may hold values from -0.75 to 0.75
- out_bias: bfloat16 [1024], P(('dp', 'fsdp')), may hold values from -3 to 3
- norm1_gain: bfloat16 [1024], P(('dp', 'fsdp')), may hold values from 0.5 to 1.5
- norm1_shift: bfloat16 [1024], P(('dp', 'fsdp')), may hold values from -3 to 3
- w_in: bfloat16 [1024, 4096], P('dp', 'fsdp'), may hold values from -0.1875 to 0.1875
- in_bias: bfloat16 [4096], P(('dp', 'fsdp')), may hold values from -3 to 3
- w_back: bfloat16 [4096, 1024], P('fsdp', 'dp'), may hold values from -0.125 to 0.125
- back_bias: bfloat16 [1024], P(('dp', 'fsdp')), may hold values from -3 to 3
- norm2_gain: bfloat16 [1024], P(('dp', 'fsdp')), may hold values from 0.5 to 1.5
- norm2_shift: bfloat16 [1024], P(('dp', 'fsdp')), may hold values from -3 to 3
- slope: float32 [16], replicated, may hold values from 0.001 to 0.08
Outputs:
- output_rows: bfloat16 [16384, 1024], P(('dp', 'fsdp'))
- input_grad: float32 [16384, 1024], P(('dp', 'fsdp'))
- grad_w_qkv: float32 [1024, 3, 1024], P('dp', None, 'fsdp')
- grad_qv_bias: float32 [2048], P(('dp', 'fsdp'))
- grad_w_out: float32 [1024, 1024], P('fsdp', 'dp')
- grad_out_bias: float32 [1024], P(('dp', 'fsdp'))
- grad_norm1_gain: float32 [1024], P(('dp', 'fsdp'))
- grad_norm1_shift: float32 [1024], P(('dp', 'fsdp'))
- grad_w_in: float32 [1024, 4096], P('dp', 'fsdp')
- grad_in_bias: float32 [4096], P(('dp', 'fsdp'))
- grad_w_back: float32 [4096, 1024], P('fsdp', 'dp')
- grad_back_bias: float32 [1024], P(('dp', 'fsdp'))
- grad_norm2_gain: float32 [1024], P(('dp', 'fsdp'))
- grad_norm2_shift: float32 [1024], P(('dp', 'fsdp'))
- grad_slope: float32 [16], replicated
The draws below stay inside these ranges and needn't reach their ends.
Inputs may be any that keep to these rules, and one draw needn't show every extreme that they name: `seq_lens`: row g lists the lengths of the sequences packed in order into group g; zeros are empty slots; each row sums to at least 512 and at most 1024, and some group holds a single sequence of 1024 rows.
All inputs are finite; a program needn't handle non-finite values.
Results may differ from the reference program's by a relative error of at most 0.02.
Values may be sent and summed in bfloat16 or wider, within the bound.
No kernel may reach another device: no remote copies, remote signals or barrier semaphores. Data moves between devices by JAX's collectives and lax.ppermute only.
A program may use at most 192 MiB of HBM per device.

```python
import math
import jax
import jax.numpy as jnp
from jax import lax

D = 1024
H = 16
HD = 64
FF = 4096
SLOTS = 4
GROUP = 1024
TOKENS = 16384
N_DP = 16


def draw_seq_lens(key, part):
    key_total, key_count, key_weight, key_full = jax.random.split(key, 4)
    group_ids = jnp.arange(N_DP, dtype=jnp.int32)
    full_group = jax.random.randint(key_full, (), 0, N_DP, dtype=jnp.int32)
    totals = jax.random.randint(key_total, (N_DP,), GROUP // 2, GROUP + 1, dtype=jnp.int32)
    totals = jnp.where(group_ids == full_group, GROUP, totals)
    counts = jax.random.randint(key_count, (N_DP,), 2, SLOTS + 1, dtype=jnp.int32)
    counts = jnp.where(group_ids == full_group, 1, counts)
    weights = jax.random.randint(key_weight, (N_DP, SLOTS), 1, 9, dtype=jnp.int32)
    slot_ids = jnp.arange(SLOTS, dtype=jnp.int32)
    weights = jnp.where(slot_ids[None, :] < counts[:, None], weights, 0)
    shares = totals[:, None] * weights // jnp.sum(weights, axis=1, keepdims=True)
    remain = totals - jnp.sum(shares, axis=1)
    shares = shares + jnp.where(slot_ids[None, :] == counts[:, None] - 1, remain[:, None], 0)
    return shares.astype(jnp.int32)


def shard_levels(own_key, shape, cuts, smallest, largest):
    def one(position, blocks):
        heights = jax.random.uniform(jax.random.fold_in(jax.random.fold_in(own_key, 6), position), (blocks,), jnp.float32, smallest / len(cuts), largest / len(cuts))
        return jnp.repeat(jnp.exp(heights), shape[position] // blocks).reshape((-1,) + (1,) * (len(shape) - position - 1))

    gain = one(*cuts[0])
    for cut in cuts[1:]:
        gain = gain * one(*cut)
    return gain


def noise(own_key, dims, deviation, reach, cuts=(), kind=jnp.bfloat16):
    gain = shard_levels(own_key, dims, cuts, -0.22, 0.18) if cuts else 1.0
    entries = jax.random.normal(own_key, dims, jnp.float32) * deviation * gain
    return jnp.minimum(jnp.maximum(entries, -reach), reach).astype(kind)


def setup_inputs(seed: int = 0) -> dict:
    streams_of = jax.random.split(jax.random.key(seed), 17)
    hidden_in = noise(streams_of[0], (TOKENS, D), 1.0, 6.0, ((0, 32),))
    cotangent = noise(streams_of[1], (TOKENS, D), 1.0, 6.0, ((0, 32),))
    seq_lens = draw_seq_lens(jax.random.fold_in(streams_of[16], 71), 0)
    w_qkv = noise(streams_of[3], (D, 3, D), D ** -0.5, 0.1875, ((0, 16), (2, 2)))
    qv_bias = noise(streams_of[4], (2 * D,), 0.5, 3.0, ((0, 32),))
    w_out = noise(streams_of[5], (D, D), (D // 16) ** -0.5, 0.75, ((0, 2), (1, 16)))
    out_bias = noise(streams_of[6], (D,), 0.5, 3.0, ((0, 32),))
    norm1_gain = jnp.clip(1.0 + 0.1 * jax.random.normal(streams_of[7], (D,), jnp.float32), 0.5, 1.5).astype(jnp.bfloat16)
    norm1_shift = noise(streams_of[8], (D,), 0.5, 3.0, ((0, 32),))
    w_in = noise(streams_of[9], (D, FF), D ** -0.5, 0.1875, ((0, 16), (1, 2)))
    in_bias = noise(streams_of[10], (FF,), 0.5, 3.0, ((0, 32),))
    w_back = noise(streams_of[11], (FF, D), (FF // 2) ** -0.5, 0.125, ((0, 2), (1, 16)))
    back_bias = noise(streams_of[12], (D,), 0.5, 3.0, ((0, 32),))
    norm2_gain = jnp.clip(1.0 + 0.1 * jax.random.normal(streams_of[13], (D,), jnp.float32), 0.5, 1.5).astype(jnp.bfloat16)
    norm2_shift = noise(streams_of[14], (D,), 0.5, 3.0, ((0, 32),))
    slope = jnp.clip(jnp.exp(jax.random.uniform(streams_of[15], (H,), jnp.float32, math.log(0.001), math.log(0.08))), 0.001, 0.08)
    return dict(hidden_in=hidden_in, cotangent=cotangent, seq_lens=seq_lens, w_qkv=w_qkv, qv_bias=qv_bias, w_out=w_out, out_bias=out_bias, norm1_gain=norm1_gain, norm1_shift=norm1_shift, w_in=w_in, in_bias=in_bias, w_back=w_back, back_bias=back_bias, norm2_gain=norm2_gain, norm2_shift=norm2_shift, slope=slope)


EPS = 1e-12
SQRT_HALF = 0.7071067811865476
INV_ROOT_TWO_PI = 0.3989422804014327

def layer_norm(hidden, gain_vec, shift_vec):
    center = hidden - lax.optimization_barrier(jnp.mean(hidden, axis=1, keepdims=True))
    inv_std = lax.rsqrt(lax.optimization_barrier(jnp.mean(center * center, axis=1, keepdims=True)) + EPS)
    normed = center * inv_std
    return (normed * gain_vec + shift_vec, normed, inv_std)

def norm_back(grad_out, normed, inv_std, gain_vec):
    grad_norm = grad_out * gain_vec
    return inv_std * (grad_norm - lax.optimization_barrier(jnp.mean(grad_norm, axis=1, keepdims=True)) - normed * lax.optimization_barrier(jnp.mean(grad_norm * normed, axis=1, keepdims=True)))

def gelu_slope(pre_act):
    return 0.5 * (1.0 + jax.scipy.special.erf(pre_act * SQRT_HALF)) + pre_act * INV_ROOT_TWO_PI * jnp.exp(-0.5 * pre_act * pre_act)

def round_half(values):
    return lax.optimization_barrier(values.astype(jnp.bfloat16))

def contract_rows(left_mat, right_mat):
    return lax.dot_general(left_mat, right_mat, (((0,), (0,)), ((), ())), preferred_element_type=jnp.float32)

def dot_trans(left_mat, right_mat):
    return lax.dot_general(left_mat, right_mat, (((1,), (1,)), ((), ())), preferred_element_type=jnp.float32)

def group_pass(hidden_in, cotangent, lengths, params):
    w_qkv, qv_bias, w_out, out_bias, norm1_gain, norm1_shift, w_in, in_bias, w_back, back_bias, norm2_gain, norm2_shift, slope = params
    w_flat = w_qkv.reshape(D, 3 * D)
    all_pos = jnp.arange(GROUP, dtype=jnp.int32)
    seq_ends = jnp.cumsum(lengths).astype(jnp.int32)
    seg_ids = lax.optimization_barrier(jnp.sum((all_pos[:, None] >= seq_ends[None, :]).astype(jnp.int32), axis=1))
    live_col = (all_pos < seq_ends[-1]).astype(jnp.float32)[:, None]
    same_seq = seg_ids[:, None] == seg_ids[None, :]
    distance = jnp.abs(all_pos[:, None] - all_pos[None, :]).astype(jnp.float32)
    qkv_rows = jnp.dot(hidden_in, w_flat, preferred_element_type=jnp.float32)
    qv_float = qv_bias.astype(jnp.float32)
    query_rows = round_half(qkv_rows[:, :D] + qv_float[:D])
    key_rows = round_half(qkv_rows[:, D:2 * D])
    value_rows = round_half(qkv_rows[:, 2 * D:] + qv_float[D:])
    q_heads = query_rows.astype(jnp.float32).reshape(GROUP, H, HD)
    k_heads = key_rows.astype(jnp.float32).reshape(GROUP, H, HD)
    v_heads = value_rows.astype(jnp.float32).reshape(GROUP, H, HD)
    scores = jnp.einsum('qhd,khd->hqk', q_heads, k_heads) * 0.125 - slope[:, None, None] * distance[None]
    scores = jnp.where(same_seq[None], scores, -1e+30)
    top_score = lax.optimization_barrier(jnp.max(scores, axis=2, keepdims=True))
    log_total = top_score + jnp.log(lax.optimization_barrier(jnp.sum(jnp.exp(scores - top_score), axis=2, keepdims=True)))
    attn_prob = jnp.exp(scores - log_total)
    probs_b = round_half(attn_prob).astype(jnp.float32)
    context = jnp.einsum('hqk,khd->qhd', probs_b, v_heads).reshape(GROUP, D).astype(jnp.bfloat16)
    res_one = hidden_in.astype(jnp.float32) + jnp.dot(context, w_out, preferred_element_type=jnp.float32) + out_bias.astype(jnp.float32)
    mid_rows, normed_one, inv_one = layer_norm(res_one, norm1_gain.astype(jnp.float32), norm1_shift.astype(jnp.float32))
    mid_b = mid_rows.astype(jnp.bfloat16)
    pre_act = jnp.dot(mid_b, w_in, preferred_element_type=jnp.float32) + in_bias.astype(jnp.float32)
    act_b = jax.nn.gelu(pre_act, approximate=False).astype(jnp.bfloat16)
    res_two = mid_rows + jnp.dot(act_b, w_back, preferred_element_type=jnp.float32) + back_bias.astype(jnp.float32)
    final_rows, normed_two, inv_two = layer_norm(res_two, norm2_gain.astype(jnp.float32), norm2_shift.astype(jnp.float32))
    output_rows = (final_rows * live_col).astype(jnp.bfloat16)
    grad_y = cotangent.astype(jnp.float32) * live_col
    d_gain_two = lax.optimization_barrier(jnp.sum(grad_y * normed_two, axis=0))
    d_shift_two = lax.optimization_barrier(jnp.sum(grad_y, axis=0))
    grad_res_two = norm_back(grad_y, normed_two, inv_two, norm2_gain.astype(jnp.float32))
    d_back_bias = lax.optimization_barrier(jnp.sum(grad_res_two, axis=0))
    grad_two_b = grad_res_two.astype(jnp.bfloat16)
    d_w_back = contract_rows(act_b, grad_two_b)
    grad_pre = dot_trans(grad_two_b, w_back) * gelu_slope(pre_act)
    d_in_bias = lax.optimization_barrier(jnp.sum(grad_pre, axis=0))
    grad_pre_b = grad_pre.astype(jnp.bfloat16)
    d_w_in = contract_rows(mid_b, grad_pre_b)
    grad_mid = grad_res_two + dot_trans(grad_pre_b, w_in)
    d_gain_one = lax.optimization_barrier(jnp.sum(grad_mid * normed_one, axis=0))
    d_shift_one = lax.optimization_barrier(jnp.sum(grad_mid, axis=0))
    grad_res_one = norm_back(grad_mid, normed_one, inv_one, norm1_gain.astype(jnp.float32))
    d_out_bias = lax.optimization_barrier(jnp.sum(grad_res_one, axis=0))
    grad_one_b = grad_res_one.astype(jnp.bfloat16)
    d_w_out = contract_rows(context, grad_one_b)
    grad_context = round_half(dot_trans(grad_one_b, w_out))
    gc_heads = grad_context.astype(jnp.float32).reshape(GROUP, H, HD)
    grad_probs = jnp.einsum('qhd,khd->hqk', gc_heads, v_heads)
    delta_rows = lax.optimization_barrier(jnp.sum(attn_prob * grad_probs, axis=2, keepdims=True))
    grad_scores = attn_prob * (grad_probs - delta_rows)
    d_slope = -lax.optimization_barrier(jnp.sum(grad_scores * distance[None], axis=(1, 2)))
    scores_b = round_half(grad_scores).astype(jnp.float32)
    grad_query = (jnp.einsum('hqk,khd->qhd', scores_b, k_heads) * 0.125).reshape(GROUP, D)
    grad_key = (jnp.einsum('hqk,qhd->khd', scores_b, q_heads) * 0.125).reshape(GROUP, D)
    grad_value = jnp.einsum('hqk,qhd->khd', probs_b, gc_heads).reshape(GROUP, D)
    d_qv_bias = jnp.concatenate([lax.optimization_barrier(jnp.sum(grad_query, axis=0)), lax.optimization_barrier(jnp.sum(grad_value, axis=0))])
    grad_qkv_b = jnp.concatenate([grad_query, grad_key, grad_value], axis=1).astype(jnp.bfloat16)
    d_w_qkv = contract_rows(hidden_in, grad_qkv_b).reshape(D, 3, D)
    input_grad = grad_res_one + dot_trans(grad_qkv_b, w_flat)
    grads = (d_w_qkv, d_qv_bias, d_w_out, d_out_bias, d_gain_one, d_shift_one, d_w_in, d_in_bias, d_w_back, d_back_bias, d_gain_two, d_shift_two, d_slope)
    return (output_rows, input_grad, grads)

def reference(hidden_in, cotangent, seq_lens, w_qkv, qv_bias, w_out, out_bias, norm1_gain, norm1_shift, w_in, in_bias, w_back, back_bias, norm2_gain, norm2_shift, slope):
    params = (w_qkv, qv_bias, w_out, out_bias, norm1_gain, norm1_shift, w_in, in_bias, w_back, back_bias, norm2_gain, norm2_shift, slope)
    blocks_in = hidden_in.reshape(N_DP, GROUP, D)
    cot_blocks = cotangent.reshape(N_DP, GROUP, D)
    grad_zero = jax.tree.map(lambda weight_arr: jnp.zeros(weight_arr.shape, jnp.float32), params)

    def group_step(running, group_items):
        block_in, block_cot, len_row = group_items
        out_block, grad_block, grads = group_pass(block_in, block_cot, len_row, params)
        summed = jax.tree.map(lambda total_grad, new_grad: total_grad + new_grad, running, grads)
        return (summed, (out_block, grad_block))
    totals, (out_blocks, grad_blocks) = lax.scan(group_step, grad_zero, (blocks_in, cot_blocks, seq_lens))
    return (out_blocks.reshape(TOKENS, D), grad_blocks.reshape(TOKENS, D), totals[0], totals[1], totals[2], totals[3], totals[4], totals[5], totals[6], totals[7], totals[8], totals[9], totals[10], totals[11], totals[12])
```

```python
import math

import jax
import jax.numpy as jnp
from jax import lax
from jax.experimental import pallas as pl
from jax.experimental.pallas import tpu as pltpu
from jax.sharding import PartitionSpec as P

EPS = 1e-12
SQRT_HALF = 0.7071067811865476
INV_ROOT_TWO_PI = 0.3989422804014327
LOG2E = 1.4426950408889634
FAR = 1e30
NT = (((1,), (1,)), ((), ()))
TN = (((0,), (0,)), ((), ()))
NN = (((1,), (0,)), ((), ()))


def layer_norm(hidden, gain_vec, shift_vec):
    center = hidden - jnp.mean(hidden, axis=1, keepdims=True)
    inv_std = lax.rsqrt(jnp.mean(center * center, axis=1, keepdims=True) + EPS)
    normed = center * inv_std
    return (normed * gain_vec + shift_vec, normed, inv_std)


def norm_back(grad_out, normed, inv_std, gain_vec):
    grad_norm = grad_out * gain_vec
    return inv_std * (
        grad_norm
        - jnp.mean(grad_norm, axis=1, keepdims=True)
        - normed * jnp.mean(grad_norm * normed, axis=1, keepdims=True)
    )


def dot(left_mat, right_mat, dims=NN):
    return lax.dot_general(left_mat, right_mat, dims, preferred_element_type=jnp.float32)


def attn_forward(qkv, far, slope2, start, rows, head_dim):
    group_rows, width = qkv[0].shape
    pair = 2 * head_dim
    pairs = width // pair
    block = math.gcd(rows, 512)
    steps = rows // block

    def kernel(start_ref, slope_ref, q_ref, k_ref, v_ref, far_ref, ctx_ref, lse_ref):
        p = pl.program_id(1)
        q = q_ref[...]
        k = k_ref[...]
        v = v_ref[...]
        low = lax.broadcasted_iota(jnp.int32, (block, pair), 1) < head_dim
        outs = []
        sums = []
        for h in range(2):
            q_head = jnp.where(low if h == 0 else ~low, q, jnp.zeros_like(q))
            scores = dot(q_head, k, NT) * (0.125 * LOG2E) - far_ref[...] * slope_ref[2 * p + h]
            top = jnp.max(scores, axis=1, keepdims=True)
            powers = jnp.exp2(scores - top)
            total = jnp.sum(powers, axis=1, keepdims=True)
            outs.append(dot(powers.astype(jnp.bfloat16), v) * (1.0 / total))
            sums.append(top + jnp.log2(total))
        ctx_ref[...] = jnp.where(low, outs[0], outs[1]).astype(jnp.bfloat16)
        lse_ref[0] = jnp.concatenate(sums, axis=1)

    return pl.pallas_call(
        kernel,
        grid_spec=pltpu.PrefetchScalarGridSpec(
            num_scalar_prefetch=2,
            grid=(steps, pairs),
            in_specs=[
                pl.BlockSpec((block, pair), lambda i, p, st, sl: (st[0] + i, p)),
                pl.BlockSpec((group_rows, pair), lambda i, p, st, sl: (0, p)),
                pl.BlockSpec((group_rows, pair), lambda i, p, st, sl: (0, p)),
                pl.BlockSpec((block, group_rows), lambda i, p, st, sl: (st[0] + i, 0)),
            ],
            out_specs=[
                pl.BlockSpec((block, pair), lambda i, p, st, sl: (i, p)),
                pl.BlockSpec((1, block, 2), lambda i, p, st, sl: (p, i, 0)),
            ],
        ),
        out_shape=[
            jax.ShapeDtypeStruct((rows, width), jnp.bfloat16),
            jax.ShapeDtypeStruct((pairs, rows, 2), jnp.float32),
        ],
        name="attn_forward",
        cost_estimate=pl.CostEstimate(
            flops=16 * rows * group_rows * width,
            transcendentals=rows * group_rows * width // head_dim,
            bytes_accessed=4 * rows * group_rows + 8 * group_rows * width,
        ),
    )((start // block).reshape(1), slope2, *qkv, far)


def attn_backward(qkv, far, slope2, grad_context, lse, start, head_dim, sums, last):
    group_rows, width = qkv[0].shape
    rows = grad_context.shape[0]
    pair = 2 * head_dim
    pairs = width // pair
    block = math.gcd(rows, 512)
    steps = rows // block
    n_sums = len(sums)

    def kernel(start_ref, slope_ref, q_ref, k_ref, v_ref, gc_ref, far_ref, lse_ref, *rest):
        sums_in = rest[:n_sums]
        dq_ref, dk_ref, dv_ref, qsum_ref, vsum_ref, ssum_ref, dk_acc, dv_acc = rest[n_sums:]
        p = pl.program_id(0)
        i = pl.program_id(1)

        @pl.when(i == 0)
        def _():
            if n_sums:
                dk_acc[...] = sums_in[0][...]
                dv_acc[...] = sums_in[1][...]
            else:
                dk_acc[...] = jnp.zeros_like(dk_acc)
                dv_acc[...] = jnp.zeros_like(dv_acc)
            qsum_ref[...] = jnp.zeros_like(qsum_ref)
            ssum_ref[...] = jnp.zeros_like(ssum_ref)

        q = q_ref[...]
        k = k_ref[...]
        v = v_ref[...]
        gc = gc_ref[...]
        low = lax.broadcasted_iota(jnp.int32, (block, pair), 1) < head_dim
        zero = jnp.zeros_like(q)
        dqs = []
        dks = []
        dvs = []
        for h in range(2):
            own = low if h == 0 else ~low
            q_head = jnp.where(own, q, zero)
            gc_head = jnp.where(own, gc, zero)
            dist = far_ref[...]
            scores = dot(k, q_head, NT) * (0.125 * LOG2E) - dist * slope_ref[2 * p + h]
            prob = jnp.exp2(scores - lse_ref[0, h : h + 1, :])
            grad_prob = dot(v, gc_head, NT)
            delta = jnp.sum(prob * grad_prob, axis=0, keepdims=True)
            grad_scores = prob * (grad_prob - delta)
            ssum_ref[0, h : h + 1, :] += jnp.sum(grad_scores * dist, axis=0, keepdims=True)
            scores_b = grad_scores.astype(jnp.bfloat16)
            dqs.append(dot(scores_b, k, TN))
            dks.append(dot(scores_b, q_head))
            dvs.append(dot(prob.astype(jnp.bfloat16), gc_head))
        grad_query = jnp.where(low, dqs[0], dqs[1]) * 0.125
        dq_ref[...] = grad_query.astype(jnp.bfloat16)
        qsum_ref[0] += jnp.sum(grad_query, axis=0, keepdims=True)
        dk_acc[...] += dks[0] + dks[1]
        dv_acc[...] += dvs[0] + dvs[1]

        @pl.when(i == steps - 1)
        def _():
            grad_value = dv_acc[...]
            if last:
                dk_ref[...] = (dk_acc[...] * 0.125).astype(jnp.bfloat16)
                dv_ref[...] = grad_value.astype(jnp.bfloat16)
            else:
                dk_ref[...] = dk_acc[...]
                dv_ref[...] = grad_value
            vsum_ref[0] = jnp.sum(grad_value, axis=0, keepdims=True)

    sum_spec = pl.BlockSpec((group_rows, pair), lambda p, i, st, sl: (0, p))
    sum_type = jax.ShapeDtypeStruct((group_rows, width), jnp.bfloat16 if last else jnp.float32)
    row_spec = pl.BlockSpec((1, 1, pair), lambda p, i, st, sl: (p, 0, 0))
    row_type = jax.ShapeDtypeStruct((pairs, 1, pair), jnp.float32)
    return pl.pallas_call(
        kernel,
        grid_spec=pltpu.PrefetchScalarGridSpec(
            num_scalar_prefetch=2,
            grid=(pairs, steps),
            in_specs=[
                pl.BlockSpec((block, pair), lambda p, i, st, sl: (st[0] + i, p)),
                pl.BlockSpec((group_rows, pair), lambda p, i, st, sl: (0, p)),
                pl.BlockSpec((group_rows, pair), lambda p, i, st, sl: (0, p)),
                pl.BlockSpec((block, pair), lambda p, i, st, sl: (i, p)),
                pl.BlockSpec((group_rows, block), lambda p, i, st, sl: (0, st[0] + i)),
                pl.BlockSpec((1, 2, block), lambda p, i, st, sl: (p, 0, i)),
            ]
            + [sum_spec] * n_sums,
            out_specs=[
                pl.BlockSpec((block, pair), lambda p, i, st, sl: (i, p)),
                sum_spec,
                sum_spec,
                row_spec,
                row_spec,
                pl.BlockSpec((1, 2, block), lambda p, i, st, sl: (p, 0, 0)),
            ],
            scratch_shapes=[pltpu.VMEM((group_rows, pair), jnp.float32)] * 2,
        ),
        out_shape=[
            jax.ShapeDtypeStruct((rows, width), jnp.bfloat16),
            sum_type,
            sum_type,
            row_type,
            row_type,
            jax.ShapeDtypeStruct((pairs, 2, block), jnp.float32),
        ],
        name="attn_backward",
        cost_estimate=pl.CostEstimate(
            flops=40 * rows * group_rows * width,
            transcendentals=rows * group_rows * width // head_dim,
            bytes_accessed=4 * rows * group_rows + 16 * group_rows * width,
        ),
    )((start // block).reshape(1), slope2, *qkv, grad_context, far, lse, *sums)


def hop(rows, shift, axis="fsdp"):
    size = lax.axis_size(axis)
    return lax.ppermute(rows, axis, [(i, (i + shift) % size) for i in range(size)])


def swap(rows, bit, axis):
    size = lax.axis_size(axis)
    return lax.ppermute(rows, axis, [(i, i ^ bit) for i in range(size)])


def bit_order(axis, turn):
    bits = [1 << j for j in range((lax.axis_size(axis) - 1).bit_length())]
    return bits[:1] + bits[2:] + bits[1:2] if turn else bits


def gather_doubling(shard, axis, turn=False):
    place = lax.axis_index(axis)
    known = []
    blocks = shard[None]
    for bit in reversed(bit_order(axis, turn)):
        inner = 1 << sum(b < bit for b in known)
        other = swap(blocks, bit, axis)
        upper = (place & bit) != 0
        mine = blocks.reshape((-1, inner) + shard.shape)
        other = other.reshape(mine.shape)
        blocks = jnp.stack(
            [jnp.where(upper, other, mine), jnp.where(upper, mine, other)], axis=1
        ).reshape((-1,) + shard.shape)
        known.append(bit)
    return blocks.reshape((-1,) + shard.shape[1:])


def scatter_halving(whole, axis, turn=False):
    size = lax.axis_size(axis)
    place = lax.axis_index(axis)
    shape = (whole.shape[0] // size,) + whole.shape[1:]
    blocks = whole.reshape((size,) + shape)
    left = bit_order(axis, False)
    for bit in bit_order(axis, turn):
        inner = 1 << sum(b < bit for b in left if b != bit)
        halves = blocks.reshape((-1, 2, inner) + shape)
        upper = jnp.where((place & bit) != 0, 1, 0)
        keep = lax.dynamic_index_in_dim(halves, upper, 1, keepdims=False)
        send = lax.dynamic_index_in_dim(halves, 1 - upper, 1, keepdims=False)
        other = swap(send.reshape((-1,) + shape), bit, axis).reshape(keep.shape)
        total = keep.astype(jnp.float32) + other.astype(jnp.float32)
        blocks = total.astype(whole.dtype).reshape((-1,) + shape)
        left.remove(bit)
    return total.reshape(shape)


def local(
    hidden_in,
    cotangent,
    seq_lens,
    w_qkv,
    qv_bias,
    w_out,
    out_bias,
    norm1_gain,
    norm1_shift,
    w_in,
    in_bias,
    w_back,
    back_bias,
    norm2_gain,
    norm2_shift,
    slope,
):
    row_count, model_width = hidden_in.shape
    member_count = lax.axis_size("fsdp")
    dp_count = lax.axis_size("dp")
    device_total = dp_count * member_count
    member = lax.axis_index("fsdp")
    group_rows = row_count * member_count
    head_count = slope.shape[0]
    head_dim = model_width // head_count
    local_heads = head_count // member_count
    local_width = local_heads * head_dim
    ff_local = w_in.shape[1]
    chunk_count = 2 if row_count % 512 == 0 else 1
    chunk = row_count // chunk_count
    float32, bfloat16 = jnp.float32, jnp.bfloat16
    members = range(member_count)

    vectors = (qv_bias, out_bias, norm1_gain, norm1_shift, in_bias, back_bias, norm2_gain, norm2_shift)
    packed = jnp.concatenate(vectors)[None]
    packed = gather_doubling(gather_doubling(packed, "fsdp"), "dp").astype(float32)
    full = []
    place = 0
    for vector in vectors:
        full.append(packed[:, place : place + vector.shape[0]].reshape(-1))
        place += vector.shape[0]
    qv_full, out_bias_full, gain_one, shift_one, in_bias_full, back_bias_full, gain_two, shift_two = full
    qkv_local = [gather_doubling(w_qkv[:, c], "dp", c == 2) for c in range(3)]
    rest = jnp.concatenate([w_in, w_back.T, w_out.T], axis=1)
    rest = lax.all_gather(rest, "dp", axis=0, tiled=True)
    in_local = rest[:, :ff_local]
    back_t = rest[:, ff_local : 2 * ff_local]
    out_t = rest[:, 2 * ff_local :]

    seq_ends = jnp.cumsum(seq_lens[0])
    all_pos = jnp.arange(group_rows, dtype=jnp.int32)
    all_seg = jnp.sum((all_pos[:, None] >= seq_ends[None, :]).astype(jnp.int32), axis=1)
    own_pos = member * row_count + jnp.arange(row_count, dtype=jnp.int32)
    live_col = (own_pos < seq_ends[-1]).astype(float32)[:, None]
    far = jnp.where(
        all_seg[:, None] == all_seg[None, :],
        jnp.abs(all_pos[:, None] - all_pos[None, :]).astype(float32),
        FAR,
    )
    slope2 = lax.dynamic_slice_in_dim(slope, member * local_heads, local_heads) * LOG2E

    def block_start(shift):
        return (member + shift + member_count) % member_count * row_count

    def in_order(blocks):
        whole = jnp.zeros((group_rows,) + blocks[0].shape[1:], blocks[0].dtype)
        for shift, part in enumerate(blocks):
            whole = lax.dynamic_update_slice_in_dim(whole, part, block_start(-shift), axis=0)
        return whole

    hidden_all = in_order([hidden_in] + [hop(hidden_in, s) for s in members[1:]])
    query_bias = lax.dynamic_slice_in_dim(qv_full, member * local_width, local_width)
    value_bias = lax.dynamic_slice_in_dim(qv_full, model_width + member * local_width, local_width)
    qkv_bias = (query_bias, 0.0, value_bias)
    qkv = [(dot(hidden_all, w) + b).astype(bfloat16) for w, b in zip(qkv_local, qkv_bias)]

    ctx_blocks = [None] * member_count
    lse_blocks = [None] * member_count
    attn_sent = []
    for ahead in list(members[1:]) + [0]:
        shift = (member_count - ahead) % member_count
        ctx, lse = attn_forward(qkv, far, slope2, block_start(ahead), row_count, head_dim)
        ctx_blocks[shift] = ctx
        lse_blocks[shift] = jnp.transpose(lse, (0, 2, 1))
        part = dot(ctx, out_t, NT)
        if ahead:
            attn_sent.append(hop(part.astype(bfloat16), ahead))
        else:
            attn_rows = part
    for part in attn_sent:
        attn_rows = attn_rows + part.astype(float32)
    res_one = hidden_in.astype(float32) + attn_rows + out_bias_full
    mid_rows, normed_one, inv_one = layer_norm(res_one, gain_one, shift_one)
    mid_b = mid_rows.astype(bfloat16)

    in_bias_local = lax.dynamic_slice_in_dim(in_bias_full, member * ff_local, ff_local)

    def spread(rows):
        parts = [rows]
        for shift in members[1:]:
            for c in range(chunk_count):
                parts.append(hop(rows[c * chunk : (c + 1) * chunk], shift))
        return parts

    def collect(parts):
        total = parts[0]
        for shift in members[1:]:
            back = [
                hop(parts[1 + (shift - 1) * chunk_count + c].astype(bfloat16), -shift)
                for c in range(chunk_count)
            ]
            total = total + jnp.concatenate(back, axis=0).astype(float32)
        return total

    def others(parts):
        return jnp.concatenate(parts[1:], axis=0)

    mid_parts = spread(mid_b)
    acts = []
    slopes = []
    ffn_parts = []
    for part in mid_parts:
        pre_act = dot(part, in_local) + in_bias_local
        below = 0.5 * (1.0 + lax.erf(pre_act * SQRT_HALF))
        acts.append((pre_act * below).astype(bfloat16))
        bell = INV_ROOT_TWO_PI * jnp.exp(-0.5 * pre_act * pre_act)
        slopes.append((below + pre_act * bell).astype(bfloat16))
        ffn_parts.append(dot(acts[-1], back_t, NT))
    res_two = mid_rows + collect(ffn_parts) + back_bias_full
    final_rows, normed_two, inv_two = layer_norm(res_two, gain_two, shift_two)
    output_rows = (final_rows * live_col).astype(bfloat16)
    grad_y = cotangent.astype(float32) * live_col
    d_gain_two = jnp.sum(grad_y * normed_two, axis=0)
    d_shift_two = jnp.sum(grad_y, axis=0)
    grad_res_two = norm_back(grad_y, normed_two, inv_two, gain_two)
    d_back_bias = jnp.sum(grad_res_two, axis=0)

    two_parts = spread(grad_res_two.astype(bfloat16))
    grad_pres = []
    d_in_local = 0.0
    back_parts = []
    for part, slope_part in zip(two_parts, slopes):
        grad_pre = dot(part, back_t) * slope_part.astype(float32)
        d_in_local = d_in_local + jnp.sum(grad_pre, axis=0)
        grad_pres.append(grad_pre.astype(bfloat16))
        back_parts.append(dot(grad_pres[-1], in_local, NT))
    d_w_back = dot(two_parts[0], acts[0], TN) + dot(others(two_parts), others(acts), TN)
    d_w_in = dot(mid_parts[0], grad_pres[0], TN) + dot(others(mid_parts), others(grad_pres), TN)
    ffn_share = jnp.concatenate([d_w_in.astype(bfloat16), d_w_back.astype(bfloat16)], axis=1)
    ffn_share, collected = lax.optimization_barrier((ffn_share, collect(back_parts)))
    ffn_share = lax.psum_scatter(ffn_share, "dp", scatter_dimension=0, tiled=True)
    grad_mid = grad_res_two + collected
    d_gain_one = jnp.sum(grad_mid * normed_one, axis=0)
    d_shift_one = jnp.sum(grad_mid, axis=0)
    grad_res_one = norm_back(grad_mid, normed_one, inv_one, gain_one)
    d_out_bias = jnp.sum(grad_res_one, axis=0)
    grad_one_b = grad_res_one.astype(bfloat16)

    one_blocks = [grad_one_b] + [hop(grad_one_b, s) for s in members[1:]]
    query_grads = []
    sums = ()
    query_sum = 0.0
    slope_sum = 0.0
    for shift in members:
        grad_context = dot(one_blocks[shift], out_t).astype(bfloat16)
        dq, dk, dv, q_sum, value_sum, s_sum = attn_backward(
            qkv,
            far,
            slope2,
            grad_context,
            lse_blocks[shift],
            block_start(-shift),
            head_dim,
            sums,
            shift == member_count - 1,
        )
        query_grads.append(dq)
        sums = (dk, dv)
        query_sum = query_sum + q_sum
        slope_sum = slope_sum - jnp.sum(s_sum, axis=2)
    d_w_out = dot(
        jnp.concatenate(one_blocks, axis=0), jnp.concatenate(ctx_blocks, axis=0), TN
    ).astype(bfloat16)
    grad_qkv = [in_order(query_grads), dk, dv]
    d_w_qkv = [dot(hidden_all, grad, TN).astype(bfloat16) for grad in grad_qkv]
    out_share = scatter_halving(d_w_out, "dp")
    qkv_shares = [scatter_halving(d_w_qkv[c], "dp", c == 0) for c in range(3)]
    input_sent = []
    for ahead in list(members[1:]) + [0]:
        part = 0.0
        for grad, w in zip(grad_qkv, qkv_local):
            rows = lax.dynamic_slice_in_dim(grad, block_start(ahead), row_count, axis=0)
            part = part + dot(rows, w, NT)
        if ahead:
            input_sent.append(hop(part.astype(bfloat16), ahead))
        else:
            input_rows = part
    for part in input_sent:
        input_rows = input_rows + part.astype(float32)
    input_grad = grad_res_one + input_rows

    def placed(size, parts):
        whole = jnp.zeros((size,), float32)
        for start, part in parts:
            whole = lax.dynamic_update_slice(whole, part, (start,))
        return whole

    qv_grad = placed(
        2 * model_width,
        (
            (member * local_width, query_sum.reshape(-1)),
            (model_width + member * local_width, value_sum.reshape(-1)),
        ),
    )
    in_grad = placed(ff_local * member_count, ((member * ff_local, d_in_local),))
    slope_grad = placed(head_count, ((member * local_heads, slope_sum.reshape(-1)),))
    grads = (qv_grad, d_out_bias, d_gain_one, d_shift_one, in_grad, d_back_bias, d_gain_two, d_shift_two)
    grads = [g.reshape(device_total, -1) for g in grads]
    table = jnp.concatenate(
        grads + [jnp.broadcast_to(slope_grad[None], (device_total, head_count))], axis=1
    )
    width = table.shape[1]
    table = scatter_halving(table, "dp").reshape(member_count, width)
    table = scatter_halving(table, "fsdp").reshape(width)
    shards = []
    place = 0
    for g in grads:
        shards.append(table[place : place + g.shape[1]])
        place += g.shape[1]
    slope_total = table[place:]

    ffn_share = ffn_share.astype(float32)
    return (
        output_rows,
        input_grad,
        jnp.stack(qkv_shares, axis=1),
        shards[0],
        out_share.T,
        shards[1],
        shards[2],
        shards[3],
        ffn_share[:, :ff_local],
        shards[4],
        ffn_share[:, ff_local:].T,
        shards[5],
        shards[6],
        shards[7],
        slope_total,
    )


def solution(mesh):
    return jax.shard_map(
        local,
        mesh=mesh,
        in_specs=(
            P(("dp", "fsdp"), None),
            P(("dp", "fsdp"), None),
            P("dp", None),
            P("dp", None, "fsdp"),
            P(("dp", "fsdp")),
            P("fsdp", "dp"),
            P(("dp", "fsdp")),
            P(("dp", "fsdp")),
            P(("dp", "fsdp")),
            P("dp", "fsdp"),
            P(("dp", "fsdp")),
            P("fsdp", "dp"),
            P(("dp", "fsdp")),
            P(("dp", "fsdp")),
            P(("dp", "fsdp")),
            P(),
        ),
        out_specs=(
            P(("dp", "fsdp"), None),
            P(("dp", "fsdp"), None),
            P("dp", None, "fsdp"),
            P(("dp", "fsdp")),
            P("fsdp", "dp"),
            P(("dp", "fsdp")),
            P(("dp", "fsdp")),
            P(("dp", "fsdp")),
            P("dp", "fsdp"),
            P(("dp", "fsdp")),
            P("fsdp", "dp"),
            P(("dp", "fsdp")),
            P(("dp", "fsdp")),
            P(("dp", "fsdp")),
            P(),
        ),
        check_vma=False,
    )
```

```python
import math

import jax
import jax.numpy as jnp
from jax import lax
from jax.experimental import pallas as pl
from jax.experimental.pallas import tpu as pltpu
from jax.sharding import PartitionSpec as P

EPS = 1e-12
SQRT_HALF = 0.7071067811865476
INV_ROOT_TWO_PI = 0.3989422804014327
LOG2E = 1.4426950408889634
FAR = 1e30
NT = (((1,), (1,)), ((), ()))
TN = (((0,), (0,)), ((), ()))
NN = (((1,), (0,)), ((), ()))


def layer_norm(hidden, gain_vec, shift_vec):
    center = hidden - jnp.mean(hidden, axis=1, keepdims=True)
    inv_std = lax.rsqrt(jnp.mean(center * center, axis=1, keepdims=True) + EPS)
    normed = center * inv_std
    return (normed * gain_vec + shift_vec, normed, inv_std)


def norm_back(grad_out, normed, inv_std, gain_vec):
    grad_norm = grad_out * gain_vec
    return inv_std * (
        grad_norm
        - jnp.mean(grad_norm, axis=1, keepdims=True)
        - normed * jnp.mean(grad_norm * normed, axis=1, keepdims=True)
    )


def dot(left_mat, right_mat, dims=NN):
    return lax.dot_general(left_mat, right_mat, dims, preferred_element_type=jnp.float32)


def attn_forward(qkv, far, slope2, start, rows, head_dim):
    group_rows, width = qkv[2].shape
    pair = 2 * head_dim
    pairs = width // pair
    block = math.gcd(rows, 512)
    steps = rows // block

    def kernel(start_ref, slope_ref, q_ref, k_ref, v_ref, far_ref, ctx_ref, lse_ref):
        p = pl.program_id(1)
        q = q_ref[...]
        k = k_ref[...]
        v = v_ref[...]
        low = lax.broadcasted_iota(jnp.int32, (block, pair), 1) < head_dim
        outs = []
        sums = []
        for h in range(2):
            q_head = jnp.where(low if h == 0 else ~low, q, jnp.zeros_like(q))
            scores = dot(q_head, k, NT) * (0.125 * LOG2E) - far_ref[...] * slope_ref[2 * p + h]
            top = jnp.max(scores, axis=1, keepdims=True)
            powers = jnp.exp2(scores - top)
            total = jnp.sum(powers, axis=1, keepdims=True)
            outs.append(dot(powers.astype(jnp.bfloat16), v) * (1.0 / total))
            sums.append(top + jnp.log2(total))
        ctx_ref[...] = jnp.where(low, outs[0], outs[1]).astype(jnp.bfloat16)
        lse_ref[0] = jnp.concatenate(sums, axis=1)

    return pl.pallas_call(
        kernel,
        grid_spec=pltpu.PrefetchScalarGridSpec(
            num_scalar_prefetch=2,
            grid=(steps, pairs),
            in_specs=[
                pl.BlockSpec((block, pair), lambda i, p, st, sl: (st[0] + i, p)),
                pl.BlockSpec((group_rows, pair), lambda i, p, st, sl: (0, pairs + p)),
                pl.BlockSpec((group_rows, pair), lambda i, p, st, sl: (0, p)),
                pl.BlockSpec((block, group_rows), lambda i, p, st, sl: (st[0] + i, 0)),
            ],
            out_specs=[
                pl.BlockSpec((block, pair), lambda i, p, st, sl: (i, p)),
                pl.BlockSpec((1, block, 2), lambda i, p, st, sl: (p, i, 0)),
            ],
        ),
        out_shape=[
            jax.ShapeDtypeStruct((rows, width), jnp.bfloat16),
            jax.ShapeDtypeStruct((pairs, rows, 2), jnp.float32),
        ],
        name="attn_forward",
        cost_estimate=pl.CostEstimate(
            flops=16 * rows * group_rows * width,
            transcendentals=rows * group_rows * width // head_dim,
            bytes_accessed=4 * rows * group_rows + 8 * group_rows * width,
        ),
    )((start // block).reshape(1), slope2, *qkv, far)


def attn_backward(qkv, far, slope2, grad_context, lse, start, head_dim, sums, last):
    group_rows, width = qkv[2].shape
    rows = grad_context.shape[0]
    pair = 2 * head_dim
    pairs = width // pair
    block = math.gcd(rows, 512)
    steps = rows // block
    n_sums = len(sums)

    def kernel(start_ref, slope_ref, q_ref, k_ref, v_ref, gc_ref, far_ref, lse_ref, *rest):
        sums_in = rest[:n_sums]
        dq_ref, dk_ref, dv_ref, qsum_ref, vsum_ref, ssum_ref, dk_acc, dv_acc = rest[n_sums:]
        p = pl.program_id(0)
        i = pl.program_id(1)

        @pl.when(i == 0)
        def _():
            if n_sums:
                dk_acc[...] = sums_in[0][...]
                dv_acc[...] = sums_in[1][...]
            else:
                dk_acc[...] = jnp.zeros_like(dk_acc)
                dv_acc[...] = jnp.zeros_like(dv_acc)
            qsum_ref[...] = jnp.zeros_like(qsum_ref)
            ssum_ref[...] = jnp.zeros_like(ssum_ref)

        q = q_ref[...]
        k = k_ref[...]
        v = v_ref[...]
        gc = gc_ref[...]
        low = lax.broadcasted_iota(jnp.int32, (block, pair), 1) < head_dim
        zero = jnp.zeros_like(q)
        dqs = []
        dks = []
        dvs = []
        for h in range(2):
            own = low if h == 0 else ~low
            q_head = jnp.where(own, q, zero)
            gc_head = jnp.where(own, gc, zero)
            dist = far_ref[...]
            scores = dot(k, q_head, NT) * (0.125 * LOG2E) - dist * slope_ref[2 * p + h]
            prob = jnp.exp2(scores - lse_ref[0, h : h + 1, :])
            grad_prob = dot(v, gc_head, NT)
            delta = jnp.sum(prob * grad_prob, axis=0, keepdims=True)
            grad_scores = prob * (grad_prob - delta)
            ssum_ref[0, h : h + 1, :] += jnp.sum(grad_scores * dist, axis=0, keepdims=True)
            scores_b = grad_scores.astype(jnp.bfloat16)
            dqs.append(dot(scores_b, k, TN))
            dks.append(dot(scores_b, q_head))
            dvs.append(dot(prob.astype(jnp.bfloat16), gc_head))
        grad_query = jnp.where(low, dqs[0], dqs[1]) * 0.125
        dq_ref[...] = grad_query.astype(jnp.bfloat16)
        qsum_ref[0] += jnp.sum(grad_query, axis=0, keepdims=True)
        dk_acc[...] += dks[0] + dks[1]
        dv_acc[...] += dvs[0] + dvs[1]

        @pl.when(i == steps - 1)
        def _():
            grad_value = dv_acc[...]
            if last:
                dk_ref[...] = (dk_acc[...] * 0.125).astype(jnp.bfloat16)
                dv_ref[...] = grad_value.astype(jnp.bfloat16)
            else:
                dk_ref[...] = dk_acc[...]
                dv_ref[...] = grad_value
            vsum_ref[0] = jnp.sum(grad_value, axis=0, keepdims=True)

    sum_spec = pl.BlockSpec((group_rows, pair), lambda p, i, st, sl: (0, p))
    sum_type = jax.ShapeDtypeStruct((group_rows, width), jnp.bfloat16 if last else jnp.float32)
    row_spec = pl.BlockSpec((1, 1, pair), lambda p, i, st, sl: (p, 0, 0))
    row_type = jax.ShapeDtypeStruct((pairs, 1, pair), jnp.float32)
    return pl.pallas_call(
        kernel,
        grid_spec=pltpu.PrefetchScalarGridSpec(
            num_scalar_prefetch=2,
            grid=(pairs, steps),
            in_specs=[
                pl.BlockSpec((block, pair), lambda p, i, st, sl: (st[0] + i, p)),
                pl.BlockSpec((group_rows, pair), lambda p, i, st, sl: (0, pairs + p)),
                pl.BlockSpec((group_rows, pair), lambda p, i, st, sl: (0, p)),
                pl.BlockSpec((block, pair), lambda p, i, st, sl: (i, p)),
                pl.BlockSpec((group_rows, block), lambda p, i, st, sl: (0, st[0] + i)),
                pl.BlockSpec((1, 2, block), lambda p, i, st, sl: (p, 0, i)),
            ]
            + [sum_spec] * n_sums,
            out_specs=[
                pl.BlockSpec((block, pair), lambda p, i, st, sl: (i, p)),
                sum_spec,
                sum_spec,
                row_spec,
                row_spec,
                pl.BlockSpec((1, 2, block), lambda p, i, st, sl: (p, 0, 0)),
            ],
            scratch_shapes=[pltpu.VMEM((group_rows, pair), jnp.float32)] * 2,
        ),
        out_shape=[
            jax.ShapeDtypeStruct((rows, width), jnp.bfloat16),
            sum_type,
            sum_type,
            row_type,
            row_type,
            jax.ShapeDtypeStruct((pairs, 2, block), jnp.float32),
        ],
        name="attn_backward",
        cost_estimate=pl.CostEstimate(
            flops=40 * rows * group_rows * width,
            transcendentals=rows * group_rows * width // head_dim,
            bytes_accessed=4 * rows * group_rows + 16 * group_rows * width,
        ),
    )((start // block).reshape(1), slope2, *qkv, grad_context, far, lse, *sums)


def hop(rows, shift, axis="fsdp"):
    size = lax.axis_size(axis)
    return lax.ppermute(rows, axis, [(i, (i + shift) % size) for i in range(size)])


def swap(rows, bit, axis):
    size = lax.axis_size(axis)
    return lax.ppermute(rows, axis, [(i, i ^ bit) for i in range(size)])


def bit_order(axis, turn):
    bits = [1 << j for j in range((lax.axis_size(axis) - 1).bit_length())]
    return bits[:1] + bits[2:] + bits[1:2] if turn else bits


def grow(blocks, known, bit, axis):
    inner = 1 << sum(b < bit for b in known)
    upper = (lax.axis_index(axis) & bit) != 0
    other = swap(blocks, bit, axis)
    mine = blocks.reshape((-1, inner) + blocks.shape[1:])
    other = other.reshape(mine.shape)
    known.append(bit)
    pair = [jnp.where(upper, other, mine), jnp.where(upper, mine, other)]
    return jnp.stack(pair, axis=1).reshape((-1,) + blocks.shape[1:])


def scatter_halving(whole, axis, turn=False):
    size = lax.axis_size(axis)
    place = lax.axis_index(axis)
    shape = (whole.shape[0] // size,) + whole.shape[1:]
    blocks = whole.reshape((size,) + shape)
    left = bit_order(axis, False)
    for bit in bit_order(axis, turn):
        inner = 1 << sum(b < bit for b in left if b != bit)
        halves = blocks.reshape((-1, 2, inner) + shape)
        upper = jnp.where((place & bit) != 0, 1, 0)
        keep = lax.dynamic_index_in_dim(halves, upper, 1, keepdims=False)
        send = lax.dynamic_index_in_dim(halves, 1 - upper, 1, keepdims=False)
        other = swap(send.reshape((-1,) + shape), bit, axis).reshape(keep.shape)
        total = keep.astype(jnp.float32) + other.astype(jnp.float32)
        blocks = total.astype(whole.dtype).reshape((-1,) + shape)
        left.remove(bit)
    return total.reshape(shape)


def local(
    hidden_in,
    cotangent,
    seq_lens,
    w_qkv,
    qv_bias,
    w_out,
    out_bias,
    norm1_gain,
    norm1_shift,
    w_in,
    in_bias,
    w_back,
    back_bias,
    norm2_gain,
    norm2_shift,
    slope,
):
    row_count, model_width = hidden_in.shape
    member_count = lax.axis_size("fsdp")
    dp_count = lax.axis_size("dp")
    device_total = dp_count * member_count
    member = lax.axis_index("fsdp")
    group_rows = row_count * member_count
    head_count = slope.shape[0]
    head_dim = model_width // head_count
    local_heads = head_count // member_count
    local_width = local_heads * head_dim
    ff_local = w_in.shape[1]
    chunk_count = 2 if row_count % 512 == 0 else 1
    chunk = row_count // chunk_count
    float32, bfloat16 = jnp.float32, jnp.bfloat16
    members = range(member_count)

    seq_ends = jnp.cumsum(seq_lens[0])
    all_pos = jnp.arange(group_rows, dtype=jnp.int32)
    all_seg = jnp.sum((all_pos[:, None] >= seq_ends[None, :]).astype(jnp.int32), axis=1)
    own_pos = member * row_count + jnp.arange(row_count, dtype=jnp.int32)
    live_col = (own_pos < seq_ends[-1]).astype(float32)[:, None]
    far = jnp.where(
        all_seg[:, None] == all_seg[None, :],
        jnp.abs(all_pos[:, None] - all_pos[None, :]).astype(float32),
        FAR,
    )

    def block_start(shift):
        return (member + shift + member_count) % member_count * row_count

    def in_order(blocks):
        whole = jnp.zeros((group_rows,) + blocks[0].shape[1:], blocks[0].dtype)
        for shift, part in enumerate(blocks):
            whole = lax.dynamic_update_slice_in_dim(whole, part, block_start(-shift), axis=0)
        return whole

    hidden_all = in_order([hidden_in] + [hop(hidden_in, s) for s in members[1:]])

    vectors = (qv_bias, out_bias, norm1_gain, norm1_shift, in_bias, back_bias, norm2_gain, norm2_shift)
    sizes = [vector.shape[0] for vector in vectors]
    packed = 0.0
    for j, vector in enumerate(vectors):
        packed = packed + jnp.pad(
            vector.astype(float32), (sum(sizes[:j]), sum(sizes[j + 1 :]))
        )
    packed = packed.astype(bfloat16)[None]
    known = []
    for bit in bit_order("fsdp", False):
        packed = grow(packed, known, bit, "fsdp")
    packed = packed[None]
    query_key = w_qkv[:, :2].reshape(1, -1, 2 * local_width)
    value_out = jnp.concatenate([w_qkv[:, 2], w_out.T], axis=1)[None]
    rest = jnp.concatenate([w_in, w_back.T], axis=1)
    known = ([], [], [])
    for bit, turned in zip(reversed(bit_order("dp", False)), reversed(bit_order("dp", True))):
        packed = grow(packed, known[0], bit, "dp")
        query_key = grow(query_key, known[1], bit, "dp")
        value_out = grow(value_out, known[2], turned, "dp")
        if len(known[0]) == 3:
            rest, hidden_all, far = lax.optimization_barrier(
                (rest, hidden_all, far, packed, query_key, value_out)
            )[:3]
    query_key = query_key.reshape(model_width, 2 * local_width)
    value_out = value_out.reshape(model_width, 2 * local_width)
    packed = packed.reshape(device_total, -1).astype(float32)
    full = []
    place = 0
    for vector in vectors:
        full.append(packed[:, place : place + vector.shape[0]].reshape(-1))
        place += vector.shape[0]
    qv_full, out_bias_full, gain_one, shift_one, in_bias_full, back_bias_full, gain_two, shift_two = full
    out_t = value_out[:, local_width:]
    qkv_local = (query_key[:, :local_width], query_key[:, local_width:], value_out[:, :local_width])
    rest = lax.all_gather(rest, "dp", axis=0, tiled=True)
    in_local = rest[:, :ff_local]
    back_t = rest[:, ff_local:]

    slope2 = lax.dynamic_slice_in_dim(slope, member * local_heads, local_heads) * LOG2E

    query_bias = lax.dynamic_slice_in_dim(qv_full, member * local_width, local_width)
    value_bias = lax.dynamic_slice_in_dim(qv_full, model_width + member * local_width, local_width)
    query_key_bias = jnp.concatenate([query_bias, jnp.zeros_like(query_bias)])
    query_key_rows = (dot(hidden_all, query_key) + query_key_bias).astype(bfloat16)
    value_rows = (dot(hidden_all, qkv_local[2]) + value_bias).astype(bfloat16)
    qkv = (query_key_rows, query_key_rows, value_rows)

    ctx_blocks = [None] * member_count
    lse_blocks = [None] * member_count
    attn_sent = []
    for ahead in list(members[1:]) + [0]:
        shift = (member_count - ahead) % member_count
        ctx, lse = attn_forward(qkv, far, slope2, block_start(ahead), row_count, head_dim)
        ctx_blocks[shift] = ctx
        lse_blocks[shift] = jnp.transpose(lse, (0, 2, 1))
        part = dot(ctx, out_t, NT)
        if ahead:
            attn_sent.append(hop(part.astype(bfloat16), ahead))
        else:
            attn_rows = part
    for part in attn_sent:
        attn_rows = attn_rows + part.astype(float32)
    res_one = hidden_in.astype(float32) + attn_rows + out_bias_full
    mid_rows, normed_one, inv_one = layer_norm(res_one, gain_one, shift_one)
    mid_b = mid_rows.astype(bfloat16)

    in_bias_local = lax.dynamic_slice_in_dim(in_bias_full, member * ff_local, ff_local)

    def spread(rows):
        parts = [rows]
        for shift in members[1:]:
            for c in range(chunk_count):
                parts.append(hop(rows[c * chunk : (c + 1) * chunk], shift))
        return parts

    def collect(parts):
        total = parts[0]
        for shift in members[1:]:
            back = [
                hop(parts[1 + (shift - 1) * chunk_count + c].astype(bfloat16), -shift)
                for c in range(chunk_count)
            ]
            total = total + jnp.concatenate(back, axis=0).astype(float32)
        return total

    def others(parts):
        return jnp.concatenate(parts[1:], axis=0)

    mid_parts = spread(mid_b)
    acts = []
    slopes = []
    ffn_parts = []
    for part in mid_parts:
        pre_act = dot(part, in_local) + in_bias_local
        below = 0.5 * (1.0 + lax.erf(pre_act * SQRT_HALF))
        acts.append((pre_act * below).astype(bfloat16))
        bell = INV_ROOT_TWO_PI * jnp.exp(-0.5 * pre_act * pre_act)
        slopes.append((below + pre_act * bell).astype(bfloat16))
        ffn_parts.append(dot(acts[-1], back_t, NT))
    res_two = mid_rows + collect(ffn_parts) + back_bias_full
    final_rows, normed_two, inv_two = layer_norm(res_two, gain_two, shift_two)
    output_rows = (final_rows * live_col).astype(bfloat16)
    grad_y = cotangent.astype(float32) * live_col
    d_gain_two = jnp.sum(grad_y * normed_two, axis=0)
    d_shift_two = jnp.sum(grad_y, axis=0)
    grad_res_two = norm_back(grad_y, normed_two, inv_two, gain_two)
    d_back_bias = jnp.sum(grad_res_two, axis=0)

    two_parts = spread(grad_res_two.astype(bfloat16))
    grad_pres = []
    d_in_local = 0.0
    back_parts = []
    for part, slope_part in zip(two_parts, slopes):
        grad_pre = dot(part, back_t) * slope_part.astype(float32)
        d_in_local = d_in_local + jnp.sum(grad_pre, axis=0)
        grad_pres.append(grad_pre.astype(bfloat16))
        back_parts.append(dot(grad_pres[-1], in_local, NT))
    d_w_back = dot(two_parts[0], acts[0], TN) + dot(others(two_parts), others(acts), TN)
    d_w_in = dot(mid_parts[0], grad_pres[0], TN) + dot(others(mid_parts), others(grad_pres), TN)
    ffn_share = jnp.concatenate([d_w_in.astype(bfloat16), d_w_back.astype(bfloat16)], axis=1)
    ffn_share, collected = lax.optimization_barrier((ffn_share, collect(back_parts)))
    ffn_share = lax.psum_scatter(ffn_share, "dp", scatter_dimension=0, tiled=True)
    grad_mid = grad_res_two + collected
    d_gain_one = jnp.sum(grad_mid * normed_one, axis=0)
    d_shift_one = jnp.sum(grad_mid, axis=0)
    grad_res_one = norm_back(grad_mid, normed_one, inv_one, gain_one)
    d_out_bias = jnp.sum(grad_res_one, axis=0)
    grad_one_b = grad_res_one.astype(bfloat16)

    one_blocks = [grad_one_b] + [hop(grad_one_b, s) for s in members[1:]]
    query_grads = []
    sums = ()
    query_sum = 0.0
    slope_sum = 0.0
    for shift in members:
        grad_context = dot(one_blocks[shift], out_t).astype(bfloat16)
        dq, dk, dv, q_sum, value_sum, s_sum = attn_backward(
            qkv,
            far,
            slope2,
            grad_context,
            lse_blocks[shift],
            block_start(-shift),
            head_dim,
            sums,
            shift == member_count - 1,
        )
        query_grads.append(dq)
        sums = (dk, dv)
        query_sum = query_sum + q_sum
        slope_sum = slope_sum - jnp.sum(s_sum, axis=2)
    d_w_out = dot(
        jnp.concatenate(one_blocks, axis=0), jnp.concatenate(ctx_blocks, axis=0), TN
    ).astype(bfloat16)
    grad_qkv = [in_order(query_grads), dk, dv]
    d_w_qkv = [dot(hidden_all, grad, TN).astype(bfloat16) for grad in grad_qkv]
    out_share = scatter_halving(d_w_out, "dp")
    qkv_shares = [scatter_halving(d_w_qkv[c], "dp", c == 0) for c in range(3)]
    input_sent = []
    for ahead in list(members[1:]) + [0]:
        part = 0.0
        for grad, w in zip(grad_qkv, qkv_local):
            rows = lax.dynamic_slice_in_dim(grad, block_start(ahead), row_count, axis=0)
            part = part + dot(rows, w, NT)
        if ahead:
            input_sent.append(hop(part.astype(bfloat16), ahead))
        else:
            input_rows = part
    for part in input_sent:
        input_rows = input_rows + part.astype(float32)
    input_grad = grad_res_one + input_rows

    def placed(size, parts):
        whole = jnp.zeros((size,), float32)
        for start, part in parts:
            whole = lax.dynamic_update_slice(whole, part, (start,))
        return whole

    qv_grad = placed(
        2 * model_width,
        (
            (member * local_width, query_sum.reshape(-1)),
            (model_width + member * local_width, value_sum.reshape(-1)),
        ),
    )
    in_grad = placed(ff_local * member_count, ((member * ff_local, d_in_local),))
    slope_grad = placed(head_count, ((member * local_heads, slope_sum.reshape(-1)),))
    grads = (qv_grad, d_out_bias, d_gain_one, d_shift_one, in_grad, d_back_bias, d_gain_two, d_shift_two)
    grads = [g.reshape(device_total, -1) for g in grads]
    table = jnp.concatenate(
        grads + [jnp.broadcast_to(slope_grad[None], (device_total, head_count))], axis=1
    )
    width = table.shape[1]
    table = scatter_halving(table, "dp").reshape(member_count, width)
    table = scatter_halving(table, "fsdp").reshape(width)
    shards = []
    place = 0
    for g in grads:
        shards.append(table[place : place + g.shape[1]])
        place += g.shape[1]
    slope_total = table[place:]

    ffn_share = ffn_share.astype(float32)
    return (
        output_rows,
        input_grad,
        jnp.stack(qkv_shares, axis=1),
        shards[0],
        out_share.T,
        shards[1],
        shards[2],
        shards[3],
        ffn_share[:, :ff_local],
        shards[4],
        ffn_share[:, ff_local:].T,
        shards[5],
        shards[6],
        shards[7],
        slope_total,
    )


def solution(mesh):
    return jax.shard_map(
        local,
        mesh=mesh,
        in_specs=(
            P(("dp", "fsdp"), None),
            P(("dp", "fsdp"), None),
            P("dp", None),
            P("dp", None, "fsdp"),
            P(("dp", "fsdp")),
            P("fsdp", "dp"),
            P(("dp", "fsdp")),
            P(("dp", "fsdp")),
            P(("dp", "fsdp")),
            P("dp", "fsdp"),
            P(("dp", "fsdp")),
            P("fsdp", "dp"),
            P(("dp", "fsdp")),
            P(("dp", "fsdp")),
            P(("dp", "fsdp")),
            P(),
        ),
        out_specs=(
            P(("dp", "fsdp"), None),
            P(("dp", "fsdp"), None),
            P("dp", None, "fsdp"),
            P(("dp", "fsdp")),
            P("fsdp", "dp"),
            P(("dp", "fsdp")),
            P(("dp", "fsdp")),
            P(("dp", "fsdp")),
            P("dp", "fsdp"),
            P(("dp", "fsdp")),
            P("fsdp", "dp"),
            P(("dp", "fsdp")),
            P(("dp", "fsdp")),
            P(("dp", "fsdp")),
            P(),
        ),
        check_vma=False,
    )
```

```python
import math

import jax
import jax.numpy as jnp
from jax import lax
from jax.experimental import pallas as pl
from jax.experimental.pallas import tpu as pltpu
from jax.sharding import PartitionSpec as P

EPS = 1e-12
SQRT_HALF = 0.7071067811865476
INV_ROOT_TWO_PI = 0.3989422804014327
LOG2E = 1.4426950408889634
FAR = 1e30
NT = (((1,), (1,)), ((), ()))
TN = (((0,), (0,)), ((), ()))
NN = (((1,), (0,)), ((), ()))


def layer_norm(hidden, gain_vec, shift_vec):
    center = hidden - jnp.mean(hidden, axis=1, keepdims=True)
    inv_std = lax.rsqrt(jnp.mean(center * center, axis=1, keepdims=True) + EPS)
    normed = center * inv_std
    return (normed * gain_vec + shift_vec, normed, inv_std)


def norm_back(grad_out, normed, inv_std, gain_vec):
    grad_norm = grad_out * gain_vec
    return inv_std * (
        grad_norm
        - jnp.mean(grad_norm, axis=1, keepdims=True)
        - normed * jnp.mean(grad_norm * normed, axis=1, keepdims=True)
    )


def dot(left_mat, right_mat, dims=NN):
    return lax.dot_general(left_mat, right_mat, dims, preferred_element_type=jnp.float32)


def attn_forward(qkv, far, slope2, start, rows, head_dim):
    group_rows, width = qkv[2].shape
    pair = 2 * head_dim
    pairs = width // pair
    block = math.gcd(rows, 512)
    steps = rows // block

    def kernel(start_ref, slope_ref, q_ref, k_ref, v_ref, far_ref, ctx_ref, lse_ref):
        p = pl.program_id(1)
        q = q_ref[...]
        k = k_ref[...]
        v = v_ref[...]
        low = lax.broadcasted_iota(jnp.int32, (block, pair), 1) < head_dim
        outs = []
        sums = []
        for h in range(2):
            q_head = jnp.where(low if h == 0 else ~low, q, jnp.zeros_like(q))
            scores = dot(q_head, k, NT) * (0.125 * LOG2E) - far_ref[...] * slope_ref[2 * p + h]
            top = jnp.max(scores, axis=1, keepdims=True)
            powers = jnp.exp2(scores - top)
            total = jnp.sum(powers, axis=1, keepdims=True)
            outs.append(dot(powers.astype(jnp.bfloat16), v) * (1.0 / total))
            sums.append(top + jnp.log2(total))
        ctx_ref[...] = jnp.where(low, outs[0], outs[1]).astype(jnp.bfloat16)
        lse_ref[0] = jnp.concatenate(sums, axis=1)

    return pl.pallas_call(
        kernel,
        grid_spec=pltpu.PrefetchScalarGridSpec(
            num_scalar_prefetch=2,
            grid=(steps, pairs),
            in_specs=[
                pl.BlockSpec((block, pair), lambda i, p, st, sl: (st[0] + i, p)),
                pl.BlockSpec((group_rows, pair), lambda i, p, st, sl: (0, pairs + p)),
                pl.BlockSpec((group_rows, pair), lambda i, p, st, sl: (0, p)),
                pl.BlockSpec((block, group_rows), lambda i, p, st, sl: (st[0] + i, 0)),
            ],
            out_specs=[
                pl.BlockSpec((block, pair), lambda i, p, st, sl: (i, p)),
                pl.BlockSpec((1, block, 2), lambda i, p, st, sl: (p, i, 0)),
            ],
        ),
        out_shape=[
            jax.ShapeDtypeStruct((rows, width), jnp.bfloat16),
            jax.ShapeDtypeStruct((pairs, rows, 2), jnp.float32),
        ],
        name="attn_forward",
        cost_estimate=pl.CostEstimate(
            flops=16 * rows * group_rows * width,
            transcendentals=rows * group_rows * width // head_dim,
            bytes_accessed=4 * rows * group_rows + 8 * group_rows * width,
        ),
    )((start // block).reshape(1), slope2, *qkv, far)


def attn_backward(qkv, far, slope2, grad_context, lse, start, head_dim, sums, last):
    group_rows, width = qkv[2].shape
    rows = grad_context.shape[0]
    pair = 2 * head_dim
    pairs = width // pair
    block = math.gcd(rows, 512)
    steps = rows // block
    n_sums = len(sums)

    def kernel(start_ref, slope_ref, q_ref, k_ref, v_ref, gc_ref, far_ref, lse_ref, *rest):
        sums_in = rest[:n_sums]
        dq_ref, dk_ref, dv_ref, qsum_ref, vsum_ref, ssum_ref, dk_acc, dv_acc = rest[n_sums:]
        p = pl.program_id(0)
        i = pl.program_id(1)

        @pl.when(i == 0)
        def _():
            if n_sums:
                dk_acc[...] = sums_in[0][...]
                dv_acc[...] = sums_in[1][...]
            else:
                dk_acc[...] = jnp.zeros_like(dk_acc)
                dv_acc[...] = jnp.zeros_like(dv_acc)
            qsum_ref[...] = jnp.zeros_like(qsum_ref)
            ssum_ref[...] = jnp.zeros_like(ssum_ref)

        q = q_ref[...]
        k = k_ref[...]
        v = v_ref[...]
        gc = gc_ref[...]
        low = lax.broadcasted_iota(jnp.int32, (block, pair), 1) < head_dim
        zero = jnp.zeros_like(q)
        dqs = []
        dks = []
        dvs = []
        for h in range(2):
            own = low if h == 0 else ~low
            q_head = jnp.where(own, q, zero)
            gc_head = jnp.where(own, gc, zero)
            dist = far_ref[...]
            scores = dot(k, q_head, NT) * (0.125 * LOG2E) - dist * slope_ref[2 * p + h]
            prob = jnp.exp2(scores - lse_ref[0, h : h + 1, :])
            grad_prob = dot(v, gc_head, NT)
            delta = jnp.sum(prob * grad_prob, axis=0, keepdims=True)
            grad_scores = prob * (grad_prob - delta)
            ssum_ref[0, h : h + 1, :] += jnp.sum(grad_scores * dist, axis=0, keepdims=True)
            scores_b = grad_scores.astype(jnp.bfloat16)
            dqs.append(dot(scores_b, k, TN))
            dks.append(dot(scores_b, q_head))
            dvs.append(dot(prob.astype(jnp.bfloat16), gc_head))
        grad_query = jnp.where(low, dqs[0], dqs[1]) * 0.125
        dq_ref[...] = grad_query.astype(jnp.bfloat16)
        qsum_ref[0] += jnp.sum(grad_query, axis=0, keepdims=True)
        dk_acc[...] += dks[0] + dks[1]
        dv_acc[...] += dvs[0] + dvs[1]

        @pl.when(i == steps - 1)
        def _():
            grad_value = dv_acc[...]
            if last:
                dk_ref[...] = (dk_acc[...] * 0.125).astype(jnp.bfloat16)
                dv_ref[...] = grad_value.astype(jnp.bfloat16)
            else:
                dk_ref[...] = dk_acc[...]
                dv_ref[...] = grad_value
            vsum_ref[0] = jnp.sum(grad_value, axis=0, keepdims=True)

    sum_spec = pl.BlockSpec((group_rows, pair), lambda p, i, st, sl: (0, p))
    sum_type = jax.ShapeDtypeStruct((group_rows, width), jnp.bfloat16 if last else jnp.float32)
    row_spec = pl.BlockSpec((1, 1, pair), lambda p, i, st, sl: (p, 0, 0))
    row_type = jax.ShapeDtypeStruct((pairs, 1, pair), jnp.float32)
    return pl.pallas_call(
        kernel,
        grid_spec=pltpu.PrefetchScalarGridSpec(
            num_scalar_prefetch=2,
            grid=(pairs, steps),
            in_specs=[
                pl.BlockSpec((block, pair), lambda p, i, st, sl: (st[0] + i, p)),
                pl.BlockSpec((group_rows, pair), lambda p, i, st, sl: (0, pairs + p)),
                pl.BlockSpec((group_rows, pair), lambda p, i, st, sl: (0, p)),
                pl.BlockSpec((block, pair), lambda p, i, st, sl: (i, p)),
                pl.BlockSpec((group_rows, block), lambda p, i, st, sl: (0, st[0] + i)),
                pl.BlockSpec((1, 2, block), lambda p, i, st, sl: (p, 0, i)),
            ]
            + [sum_spec] * n_sums,
            out_specs=[
                pl.BlockSpec((block, pair), lambda p, i, st, sl: (i, p)),
                sum_spec,
                sum_spec,
                row_spec,
                row_spec,
                pl.BlockSpec((1, 2, block), lambda p, i, st, sl: (p, 0, 0)),
            ],
            scratch_shapes=[pltpu.VMEM((group_rows, pair), jnp.float32)] * 2,
        ),
        out_shape=[
            jax.ShapeDtypeStruct((rows, width), jnp.bfloat16),
            sum_type,
            sum_type,
            row_type,
            row_type,
            jax.ShapeDtypeStruct((pairs, 2, block), jnp.float32),
        ],
        name="attn_backward",
        cost_estimate=pl.CostEstimate(
            flops=40 * rows * group_rows * width,
            transcendentals=rows * group_rows * width // head_dim,
            bytes_accessed=4 * rows * group_rows + 16 * group_rows * width,
        ),
    )((start // block).reshape(1), slope2, *qkv, grad_context, far, lse, *sums)


def weight_grads(own_in, own_back, mids, pres, twos, acts):
    depth, width = own_in.shape
    block = math.gcd(width, 1024)
    blocks = width // block
    count = len(mids)

    def kernel(in_ref, back_ref, *refs):
        out_ref = refs[4 * count]

        def add_up(total, lefts, rights):
            for left, right in zip(lefts, rights):
                total = total + dot(left[...], right[...], TN)
            out_ref[...] = total.astype(jnp.bfloat16)

        @pl.when(pl.program_id(0) < blocks)
        def _():
            add_up(in_ref[...], refs[:count], refs[count : 2 * count])

        @pl.when(pl.program_id(0) >= blocks)
        def _():
            add_up(back_ref[...], refs[2 * count : 3 * count], refs[3 * count : 4 * count])

    def first(j):
        return (0, jnp.minimum(j, blocks - 1))

    def second(j):
        return (0, jnp.maximum(j - blocks, 0))

    def whole(parts):
        return [pl.BlockSpec(part.shape, lambda j: (0, 0)) for part in parts]

    def columns(parts, place):
        return [pl.BlockSpec((part.shape[0], block), place) for part in parts]

    rows = sum(part.shape[0] for part in mids)
    return pl.pallas_call(
        kernel,
        grid=(2 * blocks,),
        in_specs=[pl.BlockSpec((depth, block), first), pl.BlockSpec((depth, block), second)]
        + whole(mids)
        + columns(pres, first)
        + whole(twos)
        + columns(acts, second),
        out_specs=pl.BlockSpec((depth, block), lambda j: (0, j)),
        out_shape=jax.ShapeDtypeStruct((depth, 2 * width), jnp.bfloat16),
        name="weight_grads",
        cost_estimate=pl.CostEstimate(
            flops=4 * rows * depth * width,
            transcendentals=0,
            bytes_accessed=12 * depth * width + 4 * rows * (depth + width),
        ),
    )(own_in, own_back, *mids, *pres, *twos, *acts)


def hop(rows, shift, axis="fsdp"):
    size = lax.axis_size(axis)
    return lax.ppermute(rows, axis, [(i, (i + shift) % size) for i in range(size)])


def swap(rows, bit, axis):
    size = lax.axis_size(axis)
    return lax.ppermute(rows, axis, [(i, i ^ bit) for i in range(size)])


def bit_order(axis, turn):
    bits = [1 << j for j in range((lax.axis_size(axis) - 1).bit_length())]
    return bits[:1] + bits[2:] + bits[1:2] if turn else bits


def grow(blocks, known, bit, axis):
    inner = 1 << sum(b < bit for b in known)
    upper = (lax.axis_index(axis) & bit) != 0
    other = swap(blocks, bit, axis)
    mine = blocks.reshape((-1, inner) + blocks.shape[1:])
    other = other.reshape(mine.shape)
    known.append(bit)
    pair = [jnp.where(upper, other, mine), jnp.where(upper, mine, other)]
    return jnp.stack(pair, axis=1).reshape((-1,) + blocks.shape[1:])


def scatter_halving(whole, axis, turn=False):
    size = lax.axis_size(axis)
    place = lax.axis_index(axis)
    shape = (whole.shape[0] // size,) + whole.shape[1:]
    blocks = whole.reshape((size,) + shape)
    left = bit_order(axis, False)
    for bit in bit_order(axis, turn):
        inner = 1 << sum(b < bit for b in left if b != bit)
        halves = blocks.reshape((-1, 2, inner) + shape)
        upper = jnp.where((place & bit) != 0, 1, 0)
        keep = lax.dynamic_index_in_dim(halves, upper, 1, keepdims=False)
        send = lax.dynamic_index_in_dim(halves, 1 - upper, 1, keepdims=False)
        other = swap(send.reshape((-1,) + shape), bit, axis).reshape(keep.shape)
        total = keep.astype(jnp.float32) + other.astype(jnp.float32)
        blocks = total.astype(whole.dtype).reshape((-1,) + shape)
        left.remove(bit)
    return total.reshape(shape)


def local(
    hidden_in,
    cotangent,
    seq_lens,
    w_qkv,
    qv_bias,
    w_out,
    out_bias,
    norm1_gain,
    norm1_shift,
    w_in,
    in_bias,
    w_back,
    back_bias,
    norm2_gain,
    norm2_shift,
    slope,
):
    row_count, model_width = hidden_in.shape
    member_count = lax.axis_size("fsdp")
    dp_count = lax.axis_size("dp")
    device_total = dp_count * member_count
    member = lax.axis_index("fsdp")
    group_rows = row_count * member_count
    head_count = slope.shape[0]
    head_dim = model_width // head_count
    local_heads = head_count // member_count
    local_width = local_heads * head_dim
    ff_local = w_in.shape[1]
    chunk_count = 2 if row_count % 512 == 0 else 1
    chunk = row_count // chunk_count
    float32, bfloat16 = jnp.float32, jnp.bfloat16
    members = range(member_count)

    seq_ends = jnp.cumsum(seq_lens[0])
    all_pos = jnp.arange(group_rows, dtype=jnp.int32)
    all_seg = jnp.sum((all_pos[:, None] >= seq_ends[None, :]).astype(jnp.int32), axis=1)
    own_pos = member * row_count + jnp.arange(row_count, dtype=jnp.int32)
    live_col = (own_pos < seq_ends[-1]).astype(float32)[:, None]
    far = jnp.where(
        all_seg[:, None] == all_seg[None, :],
        jnp.abs(all_pos[:, None] - all_pos[None, :]).astype(float32),
        FAR,
    )

    def block_start(shift):
        return (member + shift + member_count) % member_count * row_count

    def in_order(blocks):
        whole = jnp.zeros((group_rows,) + blocks[0].shape[1:], blocks[0].dtype)
        for shift, part in enumerate(blocks):
            whole = lax.dynamic_update_slice_in_dim(whole, part, block_start(-shift), axis=0)
        return whole

    hidden_all = in_order([hidden_in] + [hop(hidden_in, s) for s in members[1:]])

    vectors = (qv_bias, out_bias, norm1_gain, norm1_shift, in_bias, back_bias, norm2_gain, norm2_shift)
    sizes = [vector.shape[0] for vector in vectors]
    packed = 0.0
    for j, vector in enumerate(vectors):
        packed = packed + jnp.pad(
            vector.astype(float32), (sum(sizes[:j]), sum(sizes[j + 1 :]))
        )
    packed = packed.astype(bfloat16)[None]
    known = []
    for bit in bit_order("fsdp", False):
        packed = grow(packed, known, bit, "fsdp")
    packed = packed[None]
    query_key = w_qkv[:, :2].reshape(1, -1, 2 * local_width)
    value_out = jnp.concatenate([w_qkv[:, 2], w_out.T], axis=1)[None]
    rest = jnp.concatenate([w_in, w_back.T], axis=1)
    known = ([], [], [])
    for bit, turned in zip(reversed(bit_order("dp", False)), reversed(bit_order("dp", True))):
        packed = grow(packed, known[0], bit, "dp")
        query_key = grow(query_key, known[1], bit, "dp")
        value_out = grow(value_out, known[2], turned, "dp")
        if len(known[0]) == 3:
            rest, hidden_all, far = lax.optimization_barrier(
                (rest, hidden_all, far, packed, query_key, value_out)
            )[:3]
    query_key = query_key.reshape(model_width, 2 * local_width)
    value_out = value_out.reshape(model_width, 2 * local_width)
    packed = packed.reshape(device_total, -1).astype(float32)
    full = []
    place = 0
    for vector in vectors:
        full.append(packed[:, place : place + vector.shape[0]].reshape(-1))
        place += vector.shape[0]
    qv_full, out_bias_full, gain_one, shift_one, in_bias_full, back_bias_full, gain_two, shift_two = full
    out_t = value_out[:, local_width:]
    qkv_local = (query_key[:, :local_width], query_key[:, local_width:], value_out[:, :local_width])
    rest = lax.all_gather(rest, "dp", axis=0, tiled=True)
    in_local = rest[:, :ff_local]
    back_t = rest[:, ff_local:]

    slope2 = lax.dynamic_slice_in_dim(slope, member * local_heads, local_heads) * LOG2E

    query_bias = lax.dynamic_slice_in_dim(qv_full, member * local_width, local_width)
    value_bias = lax.dynamic_slice_in_dim(qv_full, model_width + member * local_width, local_width)
    query_key_bias = jnp.concatenate([query_bias, jnp.zeros_like(query_bias)])
    query_key_rows = (dot(hidden_all, query_key) + query_key_bias).astype(bfloat16)
    value_rows = (dot(hidden_all, qkv_local[2]) + value_bias).astype(bfloat16)
    qkv = (query_key_rows, query_key_rows, value_rows)

    ctx_blocks = [None] * member_count
    lse_blocks = [None] * member_count
    attn_sent = []
    for ahead in list(members[1:]) + [0]:
        shift = (member_count - ahead) % member_count
        ctx, lse = attn_forward(qkv, far, slope2, block_start(ahead), row_count, head_dim)
        ctx_blocks[shift] = ctx
        lse_blocks[shift] = jnp.transpose(lse, (0, 2, 1))
        part = dot(ctx, out_t, NT)
        if ahead:
            attn_sent.append(hop(part.astype(bfloat16), ahead))
        else:
            attn_rows = part
    for part in attn_sent:
        attn_rows = attn_rows + part.astype(float32)
    res_one = hidden_in.astype(float32) + attn_rows + out_bias_full
    mid_rows, normed_one, inv_one = layer_norm(res_one, gain_one, shift_one)
    mid_b = mid_rows.astype(bfloat16)

    in_bias_local = lax.dynamic_slice_in_dim(in_bias_full, member * ff_local, ff_local)

    def spread(rows):
        parts = [rows]
        for shift in members[1:]:
            for c in range(chunk_count):
                parts.append(hop(rows[c * chunk : (c + 1) * chunk], shift))
        return parts

    def collect(parts):
        total = parts[0]
        for shift in members[1:]:
            back = [
                hop(parts[1 + (shift - 1) * chunk_count + c].astype(bfloat16), -shift)
                for c in range(chunk_count)
            ]
            total = total + jnp.concatenate(back, axis=0).astype(float32)
        return total

    mid_parts = spread(mid_b)
    acts = []
    slopes = []
    ffn_parts = []
    for part in mid_parts:
        pre_act = dot(part, in_local) + in_bias_local
        below = 0.5 * (1.0 + lax.erf(pre_act * SQRT_HALF))
        acts.append((pre_act * below).astype(bfloat16))
        bell = INV_ROOT_TWO_PI * jnp.exp(-0.5 * pre_act * pre_act)
        slopes.append((below + pre_act * bell).astype(bfloat16))
        ffn_parts.append(dot(acts[-1], back_t, NT))
    res_two = mid_rows + collect(ffn_parts) + back_bias_full
    final_rows, normed_two, inv_two = layer_norm(res_two, gain_two, shift_two)
    output_rows = (final_rows * live_col).astype(bfloat16)
    grad_y = cotangent.astype(float32) * live_col
    d_gain_two = jnp.sum(grad_y * normed_two, axis=0)
    d_shift_two = jnp.sum(grad_y, axis=0)
    grad_res_two = norm_back(grad_y, normed_two, inv_two, gain_two)
    d_back_bias = jnp.sum(grad_res_two, axis=0)

    two_parts = spread(grad_res_two.astype(bfloat16))
    grad_pres = []
    d_in_local = 0.0
    back_parts = []
    for part, slope_part in zip(two_parts, slopes):
        grad_pre = dot(part, back_t) * slope_part.astype(float32)
        d_in_local = d_in_local + jnp.sum(grad_pre, axis=0)
        grad_pres.append(grad_pre.astype(bfloat16))
        back_parts.append(dot(grad_pres[-1], in_local, NT))
    ffn_share = weight_grads(
        dot(mid_parts[0], grad_pres[0], TN),
        dot(two_parts[0], acts[0], TN),
        mid_parts[1:],
        grad_pres[1:],
        two_parts[1:],
        acts[1:],
    )
    ffn_share, collected = lax.optimization_barrier((ffn_share, collect(back_parts)))
    ffn_share = lax.psum_scatter(ffn_share, "dp", scatter_dimension=0, tiled=True)
    grad_mid = grad_res_two + collected
    d_gain_one = jnp.sum(grad_mid * normed_one, axis=0)
    d_shift_one = jnp.sum(grad_mid, axis=0)
    grad_res_one = norm_back(grad_mid, normed_one, inv_one, gain_one)
    d_out_bias = jnp.sum(grad_res_one, axis=0)
    grad_one_b = grad_res_one.astype(bfloat16)

    one_blocks = [grad_one_b] + [hop(grad_one_b, s) for s in members[1:]]
    query_grads = []
    sums = ()
    query_sum = 0.0
    slope_sum = 0.0
    for shift in members:
        grad_context = dot(one_blocks[shift], out_t).astype(bfloat16)
        dq, dk, dv, q_sum, value_sum, s_sum = attn_backward(
            qkv,
            far,
            slope2,
            grad_context,
            lse_blocks[shift],
            block_start(-shift),
            head_dim,
            sums,
            shift == member_count - 1,
        )
        query_grads.append(dq)
        sums = (dk, dv)
        query_sum = query_sum + q_sum
        slope_sum = slope_sum - jnp.sum(s_sum, axis=2)
    d_w_out = dot(
        jnp.concatenate(one_blocks, axis=0), jnp.concatenate(ctx_blocks, axis=0), TN
    ).astype(bfloat16)
    grad_qkv = [in_order(query_grads), dk, dv]
    d_w_qkv = [dot(hidden_all, grad, TN).astype(bfloat16) for grad in grad_qkv]
    out_share = scatter_halving(d_w_out, "dp")
    qkv_shares = [scatter_halving(d_w_qkv[c], "dp", c == 0) for c in range(3)]
    input_sent = []
    for ahead in list(members[1:]) + [0]:
        part = 0.0
        for grad, w in zip(grad_qkv, qkv_local):
            rows = lax.dynamic_slice_in_dim(grad, block_start(ahead), row_count, axis=0)
            part = part + dot(rows, w, NT)
        if ahead:
            input_sent.append(hop(part.astype(bfloat16), ahead))
        else:
            input_rows = part
    for part in input_sent:
        input_rows = input_rows + part.astype(float32)
    input_grad = grad_res_one + input_rows

    def placed(size, parts):
        whole = jnp.zeros((size,), float32)
        for start, part in parts:
            whole = lax.dynamic_update_slice(whole, part, (start,))
        return whole

    qv_grad = placed(
        2 * model_width,
        (
            (member * local_width, query_sum.reshape(-1)),
            (model_width + member * local_width, value_sum.reshape(-1)),
        ),
    )
    in_grad = placed(ff_local * member_count, ((member * ff_local, d_in_local),))
    slope_grad = placed(head_count, ((member * local_heads, slope_sum.reshape(-1)),))
    grads = (qv_grad, d_out_bias, d_gain_one, d_shift_one, in_grad, d_back_bias, d_gain_two, d_shift_two)
    grads = [g.reshape(device_total, -1) for g in grads]
    table = jnp.concatenate(
        grads + [jnp.broadcast_to(slope_grad[None], (device_total, head_count))], axis=1
    )
    width = table.shape[1]
    table = scatter_halving(table, "dp").reshape(member_count, width)
    table = scatter_halving(table, "fsdp").reshape(width)
    shards = []
    place = 0
    for g in grads:
        shards.append(table[place : place + g.shape[1]])
        place += g.shape[1]
    slope_total = table[place:]

    ffn_share = ffn_share.astype(float32)
    return (
        output_rows,
        input_grad,
        jnp.stack(qkv_shares, axis=1),
        shards[0],
        out_share.T,
        shards[1],
        shards[2],
        shards[3],
        ffn_share[:, :ff_local],
        shards[4],
        ffn_share[:, ff_local:].T,
        shards[5],
        shards[6],
        shards[7],
        slope_total,
    )


def solution(mesh):
    return jax.shard_map(
        local,
        mesh=mesh,
        in_specs=(
            P(("dp", "fsdp"), None),
            P(("dp", "fsdp"), None),
            P("dp", None),
            P("dp", None, "fsdp"),
            P(("dp", "fsdp")),
            P("fsdp", "dp"),
            P(("dp", "fsdp")),
            P(("dp", "fsdp")),
            P(("dp", "fsdp")),
            P("dp", "fsdp"),
            P(("dp", "fsdp")),
            P("fsdp", "dp"),
            P(("dp", "fsdp")),
            P(("dp", "fsdp")),
            P(("dp", "fsdp")),
            P(),
        ),
        out_specs=(
            P(("dp", "fsdp"), None),
            P(("dp", "fsdp"), None),
            P("dp", None, "fsdp"),
            P(("dp", "fsdp")),
            P("fsdp", "dp"),
            P(("dp", "fsdp")),
            P(("dp", "fsdp")),
            P(("dp", "fsdp")),
            P("dp", "fsdp"),
            P(("dp", "fsdp")),
            P("fsdp", "dp"),
            P(("dp", "fsdp")),
            P(("dp", "fsdp")),
            P(("dp", "fsdp")),
            P(),
        ),
        check_vma=False,
    )
```
